32 devices in a mesh: dom: 8 (over y, x, core), cls: 4 (over z).
Axes of the slice: x: 2, y: 2, z: 4, core: 2. Of those that a mesh axis runs over, the one named last changes fastest.
Arguments:
- images: bfloat16 [1024, 128, 128], P(('dom', 'cls')), may hold values from -6 to 6
- class_ids: int32 [1024], P(('dom', 'cls')), may hold values from 0 to 63, as said below
- shifts: int32 [1024, 2], P(('dom', 'cls')), may hold values from -16 to 16
- defocus_bins: int32 [1024], P(('dom', 'cls')), may hold values from 0 to 31
- defocus: float32 [32], replicated, may hold values from 20 to 200
- regular: float32 [128, 128], replicated, may hold values from 1 to 32
Outputs:
- class_avg: float32 [64, 128, 128], P('cls')
The draws below stay inside these ranges and needn't reach their ends.
Inputs may be any that keep to these rules, and one draw needn't show every extreme that they name: `class_ids`: the owner of class k is k // 16. Among the 32 particles of one device exactly 16 have classes of one owner, and every other owner has at most 6 of them, exactly 6 for some; all devices with the same dom index have that same most loaded owner.
All inputs are finite; a program needn't handle non-finite values.
Results may differ from the reference program's by a relative error of at most 0.0055.
Values may be sent and summed in bfloat16 or wider, within the bound.
A program may use at most 64 MiB of HBM per device.

```python
import math
import jax
import jax.numpy as jnp
from jax import lax

SIDE = 128
STACK = 32
OWNED = 16
BINS = 32
CAPACITY = 16
PARTICLES = 1024
CLASSES = 64
N_DOM = 8
N_CLS = 4


def draw_class_ids(key, part):
    subkeys = jax.random.split(jax.random.fold_in(key, 71), 5)
    heavy_owner = jax.random.randint(subkeys[0], (N_DOM, 1, 1), 0, N_CLS)
    scores = jax.random.randint(subkeys[1], (N_DOM, N_CLS, N_CLS - 1), 0, 1 << 20) * (N_CLS - 1) + jnp.arange(N_CLS - 1, dtype=jnp.int32)
    others = jnp.argsort(scores, axis=-1).astype(jnp.int32)
    slot_ids = jnp.arange(STACK, dtype=jnp.int32)
    column = jnp.maximum(slot_ids - CAPACITY, 0) % (N_CLS - 1)
    column = jnp.broadcast_to(column, (N_DOM, N_CLS, STACK)).astype(jnp.int32)
    picked = jnp.take_along_axis(others, column, axis=-1)
    owner_of = jnp.where(slot_ids[None, None, :] < CAPACITY, heavy_owner, (heavy_owner + 1 + picked) % N_CLS)
    order_scores = jax.random.randint(subkeys[3], (N_DOM, N_CLS, STACK), 0, 1 << 20) * STACK + slot_ids
    order_ids = jnp.argsort(order_scores, axis=-1).astype(jnp.int32)
    owner_of = jnp.take_along_axis(owner_of, order_ids, axis=-1)
    within = jax.random.randint(subkeys[4], (N_DOM, N_CLS, STACK), 0, OWNED)
    return (owner_of * OWNED + within).reshape(-1).astype(jnp.int32)


def set_ends(entries, stream_key, least, high):
    spot = [jax.random.randint(jax.random.fold_in(stream_key, axis), (), 0, length) for axis, length in enumerate(entries.shape)]
    longest = entries.shape.index(max(entries.shape))
    neighbour = spot[:longest] + [(spot[longest] + 1) % entries.shape[longest]] + spot[longest + 1:]
    return entries.at[tuple(spot)].set(least).at[tuple(neighbour)].set(high)


def block_levels(own_key, dims, shards, smallest, high):
    level, own = 1.0, jax.random.fold_in(own_key, 6)
    for position, blocks in shards:
        heights = jnp.exp(jax.random.uniform(jax.random.fold_in(own, position), (blocks,), jnp.float32, smallest / len(shards), high / len(shards)))
        level = level * jnp.repeat(heights, dims[position] // blocks).reshape([-1 if axis == position else 1 for axis in range(len(dims))])
    return level


def noise(rng, dims, spread, bound, pieces=(), kind=jnp.bfloat16):
    drawn = jax.random.normal(rng, dims, jnp.float32) * spread
    if len(pieces) > 0:
        drawn = block_levels(rng, dims, pieces, -0.22, 0.18) * drawn
    return jnp.clip(drawn, min=-bound, max=bound).astype(kind)


def setup_inputs(seed: int = 0) -> dict:
    arg_keys = jax.random.split(jax.random.key(seed), 7)
    return {
        "images": noise(arg_keys[0], (PARTICLES, SIDE, SIDE), 1.0, 6.0, ((0, 32),)),
        "class_ids": draw_class_ids(jax.random.fold_in(arg_keys[6], 71), 0),
        "shifts": set_ends(jax.random.randint(arg_keys[2], (PARTICLES, 2), -(SIDE // 8), SIDE // 8 + 1), jax.random.fold_in(arg_keys[2], 1), -(SIDE // 8), (SIDE // 8 + 1) - 1).astype(jnp.int32),
        "defocus_bins": set_ends(jax.random.randint(arg_keys[3], (PARTICLES,), 0, BINS), jax.random.fold_in(arg_keys[3], 1), 0, BINS - 1).astype(jnp.int32),
        "defocus": jnp.clip(jnp.exp(jax.random.uniform(arg_keys[4], (BINS,), jnp.float32, math.log(20.0), math.log(200.0))), 20.0, 200.0),
        "regular": jnp.clip(jnp.exp(jax.random.uniform(arg_keys[5], (SIDE, SIDE), jnp.float32, math.log(1.0), math.log(32.0))), 1.0, 32.0),
    }


PHASE = 0.1
EPSILON = 1e-05

def hartley_tables(image_side):
    indices = jnp.arange(image_side, dtype=jnp.int32)
    product = indices[:, None] * indices[None, :] % image_side
    angles = product.astype(jnp.float32) * (2.0 * math.pi / image_side)
    return (jnp.cos(angles), jnp.sin(angles))

def frequency_squared(image_side):
    indices = jnp.arange(image_side, dtype=jnp.int32)
    signed = jnp.where(indices < image_side // 2, indices, indices - image_side).astype(jnp.float32) / image_side
    return signed[:, None] * signed[:, None] + signed[None, :] * signed[None, :]

def lookup(bins, defocus):
    levels = jnp.arange(defocus.shape[0], dtype=jnp.int32)
    return lax.optimization_barrier(jnp.sum(jnp.where(bins[:, None] == levels[None, :], defocus[None, :], 0.0), axis=1))

def weigh_block(pictures, offsets, bins, defocus):
    count_rows = pictures.shape[0]
    indices = jnp.arange(SIDE, dtype=jnp.int32)

    def move(picture, offset):
        return picture[(indices - offset[0]) % SIDE][:, (indices - offset[1]) % SIDE]
    shifted = jax.vmap(move)(pictures, offsets)
    cosine, sine_table = hartley_tables(SIDE)
    factor = 1.0 / math.sqrt(SIDE)
    right_table = (jnp.concatenate([cosine + sine_table, cosine - sine_table], axis=1) * factor).astype(jnp.bfloat16)
    left_table = (jnp.stack([cosine, sine_table]) * factor).astype(jnp.bfloat16)
    halves = jnp.dot(shifted.reshape(count_rows * SIDE, SIDE), right_table, preferred_element_type=jnp.float32).astype(jnp.bfloat16)
    halves = halves.reshape(count_rows, SIDE, 2, SIDE)
    spectrum = jnp.einsum('kux,pxkv->puv', left_table.astype(jnp.float32), halves.astype(jnp.float32), precision=lax.Precision.HIGHEST)
    ctf_values = -jnp.sin(lookup(bins, defocus)[:, None, None] * frequency_squared(SIDE)[None] + PHASE)
    weighted = (ctf_values * spectrum).astype(jnp.bfloat16)
    return (weighted.reshape(count_rows, SIDE * SIDE), ctf_values.reshape(count_rows, SIDE * SIDE))

def invert(average):
    classes_here = average.shape[0]
    cosine, sine_table = hartley_tables(SIDE)
    right_table = jnp.concatenate([cosine + sine_table, cosine - sine_table], axis=1)
    left_table = jnp.stack([cosine, sine_table])
    halves = jnp.dot(average.reshape(classes_here * SIDE, SIDE), right_table, precision=lax.Precision.HIGHEST)
    halves = halves.reshape(classes_here, SIDE, 2, SIDE)
    real_image = jnp.einsum('kux,pxkv->puv', left_table, halves, precision=lax.Precision.HIGHEST)
    power_mean = lax.optimization_barrier(jnp.mean(real_image * real_image, axis=(1, 2), keepdims=True))
    return real_image / jnp.sqrt(power_mean + EPSILON)

def reference(images, class_ids, shifts, defocus_bins, defocus, regular):
    group_size = PARTICLES // N_DOM
    blocks = (images.reshape(N_DOM, group_size, SIDE, SIDE), class_ids.reshape(N_DOM, group_size), shifts.reshape(N_DOM, group_size, 2), defocus_bins.reshape(N_DOM, group_size))

    def accumulate(totals, block_data):
        pictures, labels, offsets, bins = block_data
        weighted, ctf_values = weigh_block(pictures, offsets, bins, defocus)
        numerator = totals[0] + jax.ops.segment_sum(weighted.astype(jnp.float32), labels, num_segments=CLASSES)
        denominator = totals[1] + jax.ops.segment_sum(ctf_values * ctf_values, labels, num_segments=CLASSES)
        return ((numerator, denominator), None)
    start = (jnp.zeros((CLASSES, SIDE * SIDE), jnp.float32), jnp.zeros((CLASSES, SIDE * SIDE), jnp.float32))
    totals, unused = lax.scan(accumulate, start, blocks)
    average = totals[0] / (totals[1] + regular.reshape(1, SIDE * SIDE))
    return invert(average)
```

```python
import functools
import math

import jax
import jax.numpy as jnp
import numpy as np
from jax import lax
from jax.experimental import pallas as pl
from jax.experimental.pallas import tpu as pltpu
from jax.sharding import PartitionSpec as P

OWNED = 16


PHASE = 0.1
EPSILON = 1e-05


def hartley_tables(image_side):
    indices = jnp.arange(image_side, dtype=jnp.int32)
    product = indices[:, None] * indices[None, :] % image_side
    angles = product.astype(jnp.float32) * (2.0 * math.pi / image_side)
    return (jnp.cos(angles), jnp.sin(angles))


def frequency_squared(image_side):
    indices = jnp.arange(image_side, dtype=jnp.int32)
    signed = (
        jnp.where(indices < image_side // 2, indices, indices - image_side).astype(jnp.float32)
        / image_side
    )
    return signed[:, None] * signed[:, None] + signed[None, :] * signed[None, :]


def lookup(bins, defocus):
    levels = jnp.arange(defocus.shape[0], dtype=jnp.int32)
    return jnp.sum(jnp.where(bins[:, None] == levels[None, :], defocus[None, :], 0.0), axis=1)


def weigh(pictures, offsets, bins, defocus):
    count_rows = pictures.shape[0]
    image_side = pictures.shape[1]
    indices = jnp.arange(image_side, dtype=jnp.int32)
    source_rows = (indices[None, :] - offsets[:, 0:1]) % image_side
    source_cols = (indices[None, :] - offsets[:, 1:2]) % image_side
    row_select = (source_rows[:, :, None] == indices[None, None, :]).astype(jnp.bfloat16)
    col_select = (source_cols[:, :, None] == indices[None, None, :]).astype(jnp.bfloat16)
    shifted = jnp.einsum(
        "pij,pjk->pik", row_select, pictures, preferred_element_type=jnp.float32
    ).astype(jnp.bfloat16)
    shifted = jnp.einsum(
        "pik,plk->pil", shifted, col_select, preferred_element_type=jnp.float32
    ).astype(jnp.bfloat16)
    cosine, sine_table = hartley_tables(image_side)
    factor = 1.0 / math.sqrt(image_side)
    right_table = (
        jnp.concatenate([cosine + sine_table, cosine - sine_table], axis=1) * factor
    ).astype(jnp.bfloat16)
    left_table = (jnp.stack([cosine, sine_table]) * factor).astype(jnp.bfloat16)
    halves = jnp.dot(
        shifted.reshape(count_rows * image_side, image_side),
        right_table,
        preferred_element_type=jnp.float32,
    ).astype(jnp.bfloat16)
    halves = halves.reshape(count_rows, image_side, 2, image_side)
    spectrum = jnp.einsum("kux,pxkv->puv", left_table, halves, preferred_element_type=jnp.float32)
    ctf_values = -jnp.sin(
        lookup(bins, defocus)[:, None, None] * frequency_squared(image_side)[None] + PHASE
    )
    return (ctf_values * spectrum).astype(jnp.bfloat16).reshape(count_rows, image_side * image_side)


def body_general(images, class_ids, shifts, defocus_bins, defocus, regular):
    owners = lax.axis_size("cls")
    count_local = images.shape[0]
    image_side = images.shape[1]
    pixels = image_side * image_side
    capacity = min(4 * count_local // owners, count_local // 2)
    owner_of = class_ids // OWNED
    local_class = class_ids % OWNED
    member = (owner_of[:, None] == jnp.arange(owners, dtype=jnp.int32)[None, :]).astype(jnp.int32)
    before = jnp.cumsum(member, axis=0) - member
    ranked = jnp.sum(before * member, axis=1)
    slot_count = owners * capacity
    target = jnp.where(ranked < capacity, owner_of * capacity + ranked, -1)
    matches = jnp.arange(slot_count, dtype=jnp.int32)[:, None] == target[None, :]
    filled = jnp.any(matches, axis=1)
    dispatch = matches.astype(jnp.bfloat16)

    def select_ints(selection, values):
        return jnp.sum(jnp.where(selection, values[None, :], 0), axis=1)

    slot_class = jnp.where(filled, select_ints(matches, local_class), OWNED)
    slot_bin = select_ints(matches, defocus_bins)
    payload = weigh(images, shifts, defocus_bins, defocus)
    outgoing = jnp.dot(dispatch, payload, preferred_element_type=jnp.float32).astype(jnp.bfloat16)
    outgoing = outgoing.reshape(owners, capacity, pixels)
    labels = jnp.stack([slot_class, slot_bin], axis=1).reshape(owners, capacity, 2)
    arrived, arrived_labels = (
        lax.all_to_all(outgoing, "cls", split_axis=0, concat_axis=0, tiled=True),
        lax.all_to_all(labels, "cls", split_axis=0, concat_axis=0, tiled=True),
    )
    arrived_rows = arrived.reshape(slot_count, pixels)
    arrived_tags = arrived_labels.reshape(slot_count, 2)
    bin_count = defocus.shape[0]
    class_select = (jnp.arange(OWNED, dtype=jnp.int32)[:, None] == arrived_tags[None, :, 0]).astype(
        jnp.bfloat16
    )
    bin_select = (arrived_tags[:, 1:2] == jnp.arange(bin_count, dtype=jnp.int32)[None, :]).astype(
        jnp.bfloat16
    )
    numerator = jnp.dot(class_select, arrived_rows, preferred_element_type=jnp.float32)
    counts = jnp.dot(class_select, bin_select, preferred_element_type=jnp.float32)
    squared = frequency_squared(image_side).reshape(pixels)
    ctf_table = jnp.sin(defocus[:, None] * squared[None, :] + PHASE)
    ctf_table = ctf_table * ctf_table
    denominator = jnp.dot(counts, ctf_table, precision=lax.Precision.HIGHEST)
    numerator, denominator = lax.psum((numerator, denominator), "dom")
    average = numerator / (denominator + regular.reshape(1, pixels))
    cosine, sine_table = hartley_tables(image_side)
    right_table = jnp.concatenate([cosine + sine_table, cosine - sine_table], axis=1)
    left_table = jnp.stack([cosine, sine_table])
    halves = jnp.dot(
        average.reshape(OWNED * image_side, image_side),
        right_table,
        precision=lax.Precision.HIGHEST,
    )
    halves = halves.reshape(OWNED, image_side, 2, image_side)
    real_image = jnp.einsum("kux,pxkv->puv", left_table, halves, precision=lax.Precision.HIGHEST)
    power_mean = jnp.mean(real_image * real_image, axis=(1, 2), keepdims=True)
    return real_image / jnp.sqrt(power_mean + EPSILON)


HIGHEST = lax.Precision.HIGHEST
MESH = pl.DeviceIdType.MESH


def numpy_tables(side):
    indices = np.arange(side, dtype=np.int64)
    angles = (indices[:, None] * indices[None, :] % side) * (2.0 * math.pi / side)
    return np.cos(angles).astype(np.float32), np.sin(angles).astype(np.float32)


def split_table(table):
    high = table.astype(jnp.bfloat16).astype(np.float32)
    return high, table - high


def squared_row(side):
    lane = lax.broadcasted_iota(jnp.int32, (1, side), 1)
    signed = jnp.where(lane < side // 2, lane, lane - side).astype(jnp.float32) / side
    return signed * signed


def to_column(row):
    count = row.shape[1]
    first = lax.broadcasted_iota(jnp.int32, (count, count), 0)
    second = lax.broadcasted_iota(jnp.int32, (count, count), 1)
    return jnp.sum(jnp.where(first == second, row, jnp.zeros_like(row)), axis=1, keepdims=True)


def weigh_kernel(
    owners, ids_hbm, shifts_hbm, images_hbm, bins_hbm, defocus_hbm, right_hbm, left_hbm,
    part_ref, code_ref, ids_ref, shifts_ref, images_ref, bins_ref, ids_row, defocus_ref,
    right_ref, left_ref, shifted_ref, halves_ref, total_ref, arrived,
):
    count, side = images_ref.shape[0], images_ref.shape[1]
    levels = defocus_ref.shape[1]
    group = count // 4
    pairs = [
        (shifts_hbm, shifts_ref), (ids_hbm.at[0], ids_ref), (bins_hbm, bins_ref),
        (defocus_hbm, defocus_ref), (ids_hbm, ids_row),
    ]
    pairs += [
        (images_hbm.at[pl.ds(start, group)], images_ref.at[pl.ds(start, group)])
        for start in range(0, count, group)
    ]
    pairs += [(right_hbm, right_ref), (left_hbm, left_ref)]
    fetches = []
    for number, (source, target) in enumerate(pairs):
        fetches.append(pltpu.make_async_copy(source, target, arrived.at[number]))
        fetches[-1].start()
    total_ref[...] = jnp.zeros_like(total_ref)
    for copy in fetches[:5]:
        copy.wait()
    code_ref[...] = jnp.full(code_ref.shape, -1, jnp.int32)
    code_ref[:, 0:count] = ids_row[...] * levels + bins_ref[...]
    bins = to_column(bins_ref[...].astype(jnp.float32))
    level = lax.broadcasted_iota(jnp.int32, (count, levels), 1).astype(jnp.float32)
    phase_factor = jnp.sum(
        jnp.where(bins == level, defocus_ref[...], 0.0), axis=1, keepdims=True
    )
    theta = phase_factor * squared_row(side)
    sin_col, cos_col = jnp.sin(theta), jnp.cos(theta)
    sin_row = -jnp.sin(theta + PHASE).T
    cos_row = -jnp.cos(theta + PHASE).T
    for p in range(count):
        if p % group == 0:
            fetches[5 + p // group].wait()
        picture = images_ref[p].astype(jnp.float32)
        picture = pltpu.roll(picture, lax.rem(shifts_ref[1, p] + side, side), 1)
        picture = pltpu.roll(picture, lax.rem(shifts_ref[0, p] + side, side), 0)
        shifted_ref[p] = picture.astype(jnp.bfloat16)
    fetches[-2].wait()
    halves_ref[...] = jnp.dot(
        shifted_ref[...].reshape(count * side, side),
        right_ref[...],
        preferred_element_type=jnp.float32,
    ).astype(jnp.bfloat16)
    fetches[-1].wait()
    for p in range(count):
        block = halves_ref[pl.ds(p * side, side), :]
        stacked = jnp.concatenate([block[:, :side], block[:, side:]], axis=0)
        spectrum = jnp.dot(left_ref[...], stacked, preferred_element_type=jnp.float32)
        ctf = (
            sin_row[:, p : p + 1] * cos_col[p : p + 1, :]
            + cos_row[:, p : p + 1] * sin_col[p : p + 1, :]
        )
        label = ids_ref[p]
        slot = lax.rem(label, OWNED) * owners + lax.div(label, OWNED)
        total_ref[slot] += ctf * spectrum
    part_ref[...] = total_ref[...].astype(jnp.bfloat16)


def split_high_low(values):
    high = values.astype(jnp.bfloat16)
    return high, (values - high.astype(jnp.float32)).astype(jnp.bfloat16)


def merge_kernel(
    part_hbm, code_ref, defocus_hbm, regular_hbm, right_hbm, left_hbm, out_ref,
    part_ref, defocus_ref, regular_ref, right_ref, left_ref,
    codes, got_c, got_a1, got_b1, got_a2, got_b2, got_z,
    put_a1, put_b1, put_a2, put_b2, put_z, sent, landed, arrived,
):
    owners, side = part_hbm.shape[4], part_hbm.shape[5]
    levels = defocus_ref.shape[1]
    dom, z = lax.axis_index("dom"), lax.axis_index("cls")
    y, x, c = dom // 4, dom // 2 % 2, dom % 2
    ny, nx, nc = 1 - y, 1 - x, 1 - c
    to_core = (dom + 1 - 2 * c, z)
    to_x = (dom + 2 * (1 - 2 * x), z)
    to_y = (dom + 4 * (1 - 2 * y), z)
    steps = sorted(range(1, owners), key=lambda step: -min(step, owners - step))
    to_z = [(dom, lax.rem(z + step, owners)) for step in steps]
    codes[z, y, x, c] = code_ref[...]
    barrier = pltpu.get_barrier_semaphore()
    for partner in [to_core, to_x, to_y] + to_z:
        pl.semaphore_signal(barrier, inc=1, device_id=partner, device_id_type=MESH)
    order = [lax.rem(z + step, owners) for step in steps] + [z]
    last = owners - 1
    fetches = []
    for number, (source, target) in enumerate(
        [(defocus_hbm, defocus_ref)]
        + [(part_hbm.at[:, :, c, :, owner], part_ref.at[:, :, :, owner]) for owner in order]
        + [(regular_hbm, regular_ref), (right_hbm, right_ref), (left_hbm, left_ref)]
    ):
        fetches.append(pltpu.make_async_copy(source, target, arrived.at[number]))
        fetches[-1].start()
    issued = []

    def send(source, target, device):
        number = len(issued)
        copy = pltpu.make_async_remote_copy(
            src_ref=source,
            dst_ref=target,
            send_sem=sent.at[number],
            recv_sem=landed.at[number],
            device_id=device,
            device_id_type=MESH,
        )
        copy.start()
        issued.append(copy)
        return copy

    pl.semaphore_wait(barrier, 2 + owners)

    own_codes = codes.at[z, y, x, c]
    c_t = send(own_codes, own_codes, to_core)
    c_all = [
        send(part_hbm.at[:, :, nc, :, owner], got_c.at[:, :, :, owner], to_core)
        for owner in order
    ]
    a1, b1, a2, b2, z_all = {}, {}, {}, {}, []

    def pair(row, column, j, owner):
        own = part_ref[row, column, j, owner].astype(jnp.float32)
        return own + got_c[row, column, j, owner].astype(jnp.float32)

    def first(i):
        owner = order[i]
        fetches[1 + i].wait()
        c_all[i].wait_recv()
        put_a1[i, 0] = pair(ny, nx, 0, owner).astype(jnp.bfloat16)
        put_a1[i, 1] = pair(y, nx, 0, owner).astype(jnp.bfloat16)
        a1[i] = send(put_a1.at[i], got_a1.at[i], to_x)
        put_b1[i, 0] = pair(ny, nx, 1, owner).astype(jnp.bfloat16)
        put_b1[i, 1] = pair(ny, x, 1, owner).astype(jnp.bfloat16)
        b1[i] = send(put_b1.at[i], got_b1.at[i], to_y)

    def second(i):
        owner = order[i]
        a1[i].wait_recv()
        put_a2[i] = (pair(ny, x, 0, owner) + got_a1[i, 0].astype(jnp.float32)).astype(jnp.bfloat16)
        a2[i] = send(put_a2.at[i], got_a2.at[i], to_y)
        b1[i].wait_recv()
        put_b2[i] = (pair(y, nx, 1, owner) + got_b1[i, 0].astype(jnp.float32)).astype(jnp.bfloat16)
        b2[i] = send(put_b2.at[i], got_b2.at[i], to_x)

    def merged(i):
        owner = order[i]
        a2[i].wait_recv()
        b2[i].wait_recv()
        one = pair(y, x, 0, owner) + got_a1[i, 1].astype(jnp.float32)
        two = pair(y, x, 1, owner) + got_b1[i, 1].astype(jnp.float32)
        return one + got_a2[i].astype(jnp.float32), two + got_b2[i].astype(jnp.float32)

    def third(i):
        one, two = merged(i)
        put_z[i, 0] = one.astype(jnp.bfloat16)
        put_z[i, 1] = two.astype(jnp.bfloat16)
        z_all.append(send(put_z.at[i], got_z.at[i], to_z[i]))

    for i in range(last):
        first(i)
    fetches[0].wait()
    squared = squared_row(side)
    double = 2.0 * to_column(defocus_ref[...]) * squared
    across = jnp.concatenate([jnp.cos(double), jnp.sin(double)], axis=0)
    cos_down = jnp.cos(double + 2.0 * PHASE)
    sin_down = jnp.sin(double + 2.0 * PHASE)
    c_t.wait()
    x_t = send(codes.at[z, y, x], codes.at[z, y, x], to_x)
    second(0)
    first(last)
    x_t.wait()
    y_t = send(codes.at[z, y], codes.at[z, y], to_y)
    for i in range(1, last):
        second(i)
    third(0)
    y_t.wait()
    waits_t = [send(codes.at[z], codes.at[z], partner) for partner in to_z]
    second(last)
    for i in range(1, last):
        third(i)
    for copy in waits_t:
        copy.wait()
    level = lax.broadcasted_iota(jnp.int32, (levels, codes.shape[-1]), 0)
    rows = [
        codes[a, b // 4, b // 2 % 2, b % 2] for a in range(owners) for b in range(8)
    ]
    fetches[1 + owners].wait()
    divisors = []
    for j in range(2):
        wanted = level + (z * OWNED + dom * 2 + j) * levels
        hits = jnp.zeros(level.shape, jnp.float32)
        for row in rows:
            hits = hits + jnp.where(row == wanted, 1.0, 0.0)
        counts = jnp.sum(hits, axis=1, keepdims=True)
        down = jnp.concatenate([counts * cos_down, -(counts * sin_down)], axis=0)
        doubled = lax.dot_general(
            down, across, (((0,), (0,)), ((), ())),
            precision=HIGHEST, preferred_element_type=jnp.float32,
        )
        divisors.append(0.5 * (jnp.sum(counts) - doubled) + regular_ref[...])
    numerators = list(merged(last))
    fetches[2 + owners].wait()
    fetches[3 + owners].wait()
    for i in range(last):
        z_all[i].wait_recv()
        for j in range(2):
            numerators[j] = numerators[j] + got_z[i, j].astype(jnp.float32)
    average = jnp.concatenate([numerators[j] / divisors[j] for j in range(2)], axis=0)
    high, low = split_high_low(average)
    halves = jnp.dot(
        jnp.concatenate([high, high, low], axis=1), right_ref[...],
        preferred_element_type=jnp.float32,
    )
    for j in range(2):
        mine = halves[j * side : (j + 1) * side]
        high, low = split_high_low(
            jnp.concatenate([mine[:, :side], mine[:, side:]], axis=0)
        )
        real_image = jnp.dot(
            left_ref[...], jnp.concatenate([high, high, low], axis=0),
            preferred_element_type=jnp.float32,
        )
        power_mean = jnp.sum(real_image * real_image) / (side * side)
        scaled = real_image / jnp.sqrt(jnp.full((1, side), power_mean + EPSILON))
        out_ref[y, x, c, j] = scaled.astype(jnp.bfloat16)

    def spread(row, column, j, device):
        where = out_ref.at[row, column, c, j]
        return send(where, where, device)

    near_a = spread(y, x, 0, to_x)
    near_b = spread(y, x, 1, to_y)
    side_a = spread(y, x, 0, to_y)
    side_b = spread(y, x, 1, to_x)
    ends = [send(out_ref.at[y, x, c], out_ref.at[y, x, c], to_core)]
    near_a.wait_recv()
    far_a = spread(y, nx, 0, to_y)
    ends.append(spread(y, nx, 0, to_core))
    near_b.wait_recv()
    far_b = spread(ny, x, 1, to_x)
    ends.append(spread(ny, x, 1, to_core))
    side_a.wait_recv()
    ends.append(spread(ny, x, 0, to_core))
    side_b.wait_recv()
    ends.append(spread(y, nx, 1, to_core))
    far_a.wait_recv()
    ends.append(spread(ny, nx, 0, to_core))
    far_b.wait_recv()
    ends.append(spread(ny, nx, 1, to_core))
    for copy in ends:
        copy.wait_recv()
    tags = {id(copy) for copy in [c_t, x_t, y_t] + waits_t}
    for copy in issued:
        if id(copy) not in tags:
            copy.wait_send()


def widen_kernel(half_hbm, full_hbm, half_ref, full_ref, arrived, stored):
    pieces = arrived.shape[0]
    rows = half_ref.shape[0] // pieces
    windows = [pl.ds(piece * rows, rows) for piece in range(pieces)]
    fetches = [
        pltpu.make_async_copy(half_hbm.at[window], half_ref.at[window], arrived.at[piece])
        for piece, window in enumerate(windows)
    ]
    stores = [
        pltpu.make_async_copy(full_ref.at[window], full_hbm.at[window], stored.at[piece])
        for piece, window in enumerate(windows)
    ]
    for copy in fetches:
        copy.start()
    for piece, window in enumerate(windows):
        fetches[piece].wait()
        full_ref[window] = half_ref[window].astype(jnp.float32)
        stores[piece].start()
    for copy in stores:
        copy.wait()


def body_cube(images, class_ids, shifts, defocus_bins, defocus, regular):
    owners = lax.axis_size("cls")
    count, side = images.shape[0], images.shape[1]
    classes = owners * OWNED
    levels = defocus.shape[0]
    cosine, sine = numpy_tables(side)
    scale = np.float32(1.0 / math.sqrt(side))
    right = np.concatenate([cosine + sine, cosine - sine], axis=1)
    left = np.concatenate([cosine, sine], axis=1)
    right_high, right_low = split_table(right)
    left_high, left_low = split_table(left)
    vmem = pl.BlockSpec(memory_space=pltpu.VMEM)
    hbm = pl.BlockSpec(memory_space=pltpu.HBM)
    ids_row = class_ids.reshape(1, count)
    bins_row = defocus_bins.reshape(1, count)
    defocus_row = defocus.reshape(1, levels)
    half, full = jnp.bfloat16, jnp.float32
    part, code = pl.pallas_call(
        functools.partial(weigh_kernel, owners),
        out_shape=(
            jax.ShapeDtypeStruct((classes, side, side), half),
            jax.ShapeDtypeStruct((1, 128), jnp.int32),
        ),
        in_specs=[hbm] * 7,
        out_specs=(vmem, vmem),
        scratch_shapes=[
            pltpu.SMEM((count,), jnp.int32),
            pltpu.SMEM((2, count), jnp.int32),
            pltpu.VMEM((count, side, side), half),
            pltpu.VMEM((1, count), jnp.int32),
            pltpu.VMEM((1, count), jnp.int32),
            pltpu.VMEM((1, levels), full),
            pltpu.VMEM((side, 2 * side), half),
            pltpu.VMEM((side, 2 * side), half),
            pltpu.VMEM((count, side, side), half),
            pltpu.VMEM((count * side, 2 * side), half),
            pltpu.VMEM((classes, side, side), full),
            pltpu.SemaphoreType.DMA((11,)),
        ],
        compiler_params=pltpu.CompilerParams(vmem_limit_bytes=60 * 1024 * 1024),
        name="weigh",
    )(
        ids_row, shifts.T, images, bins_row, defocus_row,
        jnp.asarray(right * scale).astype(half),
        jnp.asarray(left * scale).astype(half),
    )
    copies = 1 + 5 * owners + 2 + 2 * (owners - 1) + 13
    block = (side, side)
    merged = pl.pallas_call(
        merge_kernel,
        out_shape=jax.ShapeDtypeStruct((2, 2, 2, 2) + block, half),
        in_specs=[hbm, vmem, hbm, hbm, hbm, hbm],
        out_specs=vmem,
        scratch_shapes=[
            pltpu.VMEM((2, 2, 2, owners) + block, half),
            pltpu.VMEM((1, levels), full),
            pltpu.VMEM(block, full),
            pltpu.VMEM((3 * side, 2 * side), half),
            pltpu.VMEM((side, 6 * side), half),
            pltpu.VMEM((owners, 2, 2, 2, 1, 128), jnp.int32),
            pltpu.VMEM((2, 2, 2, owners) + block, half),
            pltpu.VMEM((owners, 2) + block, half),
            pltpu.VMEM((owners, 2) + block, half),
            pltpu.VMEM((owners,) + block, half),
            pltpu.VMEM((owners,) + block, half),
            pltpu.VMEM((owners - 1, 2) + block, half),
            pltpu.VMEM((owners, 2) + block, half),
            pltpu.VMEM((owners, 2) + block, half),
            pltpu.VMEM((owners,) + block, half),
            pltpu.VMEM((owners,) + block, half),
            pltpu.VMEM((owners - 1, 2) + block, half),
            pltpu.SemaphoreType.DMA((copies,)),
            pltpu.SemaphoreType.DMA((copies,)),
            pltpu.SemaphoreType.DMA((4 + owners,)),
        ],
        compiler_params=pltpu.CompilerParams(
            collective_id=0, has_side_effects=True, vmem_limit_bytes=60 * 1024 * 1024
        ),
        name="merge",
    )(
        part.reshape((2, 2, 2, 2, owners) + block), code, defocus_row, regular,
        jnp.asarray(np.concatenate([right_high, right_low, right_high], axis=0)).astype(half),
        jnp.asarray(np.concatenate([left_high, left_low, left_high], axis=1)).astype(half),
    )
    return pl.pallas_call(
        widen_kernel,
        out_shape=jax.ShapeDtypeStruct((OWNED,) + block, full),
        in_specs=[hbm],
        out_specs=hbm,
        scratch_shapes=[
            pltpu.VMEM((OWNED,) + block, half),
            pltpu.VMEM((OWNED,) + block, full),
            pltpu.SemaphoreType.DMA((4,)),
            pltpu.SemaphoreType.DMA((4,)),
        ],
        compiler_params=pltpu.CompilerParams(vmem_limit_bytes=60 * 1024 * 1024),
        name="widen",
    )(merged.reshape((OWNED,) + block))


def solution(mesh):
    in_specs = (
        P(("dom", "cls"), None, None),
        P(("dom", "cls")),
        P(("dom", "cls"), None),
        P(("dom", "cls")),
        P(),
        P(),
    )
    cube = mesh.shape["dom"] == 8 and OWNED == 2 * mesh.shape["dom"]
    body = body_cube if cube else body_general
    out_specs = P("cls", None, None)
    return jax.shard_map(body, mesh=mesh, in_specs=in_specs, out_specs=out_specs, check_vma=False)
```
